32 devices in a mesh: fsdp: 8 (over z, x), rep: 4 (over y, core).
Axes of the slice: x: 2, y: 2, z: 4, core: 2. Of those that a mesh axis runs over, the one named last changes fastest.
Arguments:
- tokens_x: bfloat16 [4096, 8192], P(('fsdp', 'rep')), may hold values from -6 to 6
- cotangent: bfloat16 [4096, 128], P(('fsdp', 'rep')), may hold values from -1 to 1
- master_weight: float32 [8192, 128], P('fsdp'), may hold values from -0.015625 to 0.015625
- first_moment: float32 [8192, 128], P('fsdp'), may hold values from -6 to 6
- second_moment: float32 [8192, 128], P('fsdp'), may hold values from 0.5 to 2
- hidden_dec: bfloat16 [2, 64, 8192], P(None, ('fsdp', 'rep')), may hold values from -6 to 6
- queries: bfloat16 [2, 64, 1024], P(None, ('fsdp', 'rep')), may hold values from -64 to 64
- new_values: bfloat16 [2, 64, 128], P(None, ('fsdp', 'rep')), may hold values from -6 to 6
- key_cache: bfloat16 [64, 1024, 128], P(('fsdp', 'rep')), may hold values from -64 to 64
- value_cache: bfloat16 [64, 1024, 128], P(('fsdp', 'rep')), may hold values from -6 to 6
- cache_lengths: int32 [64], P(('fsdp', 'rep')), may hold values from 2 to 1022, as said below
Outputs:
- weight_next: float32 [8192, 128], P('fsdp')
- first_next: float32 [8192, 128], P('fsdp')
- second_next: float32 [8192, 128], P('fsdp')
- rollout_weight: bfloat16 [8192, 128], replicated
- fresh_keys: bfloat16 [2, 64, 128], P(None, ('fsdp', 'rep'))
- attended: bfloat16 [2, 64, 1024], P(None, ('fsdp', 'rep'))
The draws below stay inside these ranges and needn't reach their ends.
Inputs may be any that keep to these rules, and one draw needn't show every extreme that they name: `cache_lengths`: some row has exactly 1022 filled slots.
All inputs are finite; a program needn't handle non-finite values. Where the reference program divides by a largest or mean magnitude, that divisor is 1e-20 or more.
Results may differ from the reference program's by a relative error of at most 0.0049.
Values may be sent and summed in bfloat16 or wider, within the bound.
A program may use at most 64 MiB of HBM per device.

```python
import math
import jax
import jax.numpy as jnp
from jax import lax

D = 8192
HD = 128
QPK = 8
CACHE = 1024
STEPS = 2
BLOCK = 128
TOKENS = 4096
ROWS = 64


def draw_queries(key, part):
    result = jnp.clip(jax.random.normal(jax.random.fold_in(key, 11), (STEPS, ROWS, QPK * HD), jnp.float32), -6.0, 6.0)
    return result.astype(jnp.bfloat16)


def draw_key_cache(key, part):
    result = jnp.clip(jax.random.normal(jax.random.fold_in(key, 13), (ROWS, CACHE, HD), jnp.float32), -6.0, 6.0)
    return result.astype(jnp.bfloat16)


def draw_cache_lengths(key, part):
    filled = jax.random.randint(jax.random.fold_in(key, 17), (ROWS,), 2, CACHE - STEPS + 1, jnp.int32)
    longest = jax.random.randint(jax.random.fold_in(key, 19), (), 0, ROWS, jnp.int32)
    return jnp.where(jnp.arange(ROWS, dtype=jnp.int32) == longest, CACHE - STEPS, filled).astype(jnp.int32)


def with_spikes(values, own_key, source, target, shards_of, factor):
    def block_of(position):
        return (jnp.arange(values.shape[position]) // (values.shape[position] // shards_of)).reshape((-1,) + (1,) * (values.ndim - 1 - position))

    one_side = jax.random.permutation(own_key, shards_of)[block_of(target)]
    second = (block_of(target) + shards_of // 2) % shards_of
    return jnp.where((block_of(source) == one_side) | (block_of(source) == second), factor * values, values)


def block_scale(stream_key, dims, cuts, least, high):
    def one(position, parts):
        draws = jax.random.uniform(jax.random.fold_in(jax.random.fold_in(stream_key, 6), position), (parts,), jnp.float32, least / len(cuts), high / len(cuts))
        return jnp.repeat(jnp.exp(draws), dims[position] // parts).reshape((-1,) + (1,) * (len(dims) - position - 1))

    loudness = one(*cuts[0])
    for cut in cuts[1:]:
        loudness = loudness * one(*cut)
    return loudness


def bell_draw(stream_key, dims, scale, limit, pieces=(), kind=jnp.bfloat16):
    gain = block_scale(stream_key, dims, pieces, -0.22, 0.18) if pieces else 1.0
    values = jax.random.normal(stream_key, dims, jnp.float32) * scale * gain
    return jnp.minimum(jnp.maximum(values, -limit), limit).astype(kind)


def gaussian_with(key, shape, scale, limit, pieces, heavy, kind=jnp.bfloat16):
    drawn = scale * jax.random.normal(key, shape, jnp.float32)
    if pieces:
        drawn = drawn * block_scale(key, shape, pieces, -0.22, 0.18)
    return jnp.clip(with_spikes(drawn, jax.random.fold_in(key, 3), *heavy), -limit, limit).astype(kind)


def setup_inputs(seed: int = 0) -> dict:
    arg_keys = jax.random.split(jax.random.key(seed), 12)
    tokens_x = gaussian_with(arg_keys[0], (TOKENS, D), 1.0, 6.0, ((0, 32),), (0, 1, 32, 2.75))
    cotangent = bell_draw(arg_keys[1], (TOKENS, HD), (max(TOKENS // 100, 1)) ** -0.5, 1.0, ((0, 32),))
    master_weight = bell_draw(arg_keys[2], (D, HD), (16 * D) ** -0.5, 0.015625, ((0, 8),), jnp.float32)
    first_moment = bell_draw(arg_keys[3], (D, HD), 1.0, 6.0, ((0, 8),), jnp.float32)
    second_moment = jnp.clip(jnp.exp(math.log(2.0) - 1.3862944 * jax.random.uniform(arg_keys[4], (D, HD), jnp.float32) ** block_scale(arg_keys[4], (D, HD), ((0, 8),), -0.2, 0.2)), 0.5, 2.0)
    hidden_dec = bell_draw(arg_keys[5], (STEPS, ROWS, D), 1.0, 6.0, ((1, 32),))
    queries = draw_queries(jax.random.fold_in(arg_keys[11], 71), 0)
    new_values = bell_draw(arg_keys[7], (STEPS, ROWS, HD), 1.0, 6.0, ((1, 32),))
    key_cache = draw_key_cache(jax.random.fold_in(arg_keys[11], 71), 0)
    value_cache = bell_draw(arg_keys[9], (ROWS, CACHE, HD), 1.0, 6.0, ((0, 32),))
    cache_lengths = draw_cache_lengths(jax.random.fold_in(arg_keys[11], 71), 0)
    return dict(tokens_x=tokens_x, cotangent=cotangent, master_weight=master_weight, first_moment=first_moment, second_moment=second_moment, hidden_dec=hidden_dec, queries=queries, new_values=new_values, key_cache=key_cache, value_cache=value_cache, cache_lengths=cache_lengths)


beta_one = 0.9
beta_two = 0.95
adam_eps = 1e-08
learn_rate = 0.0003
weight_decay = 0.1
step_count = 100
rope_theta = 1000000.0
peak_eps = 1e-06

def adamw(weight, first, second, gradient):
    first_new = beta_one * first + (1.0 - beta_one) * gradient
    second_new = beta_two * second + (1.0 - beta_two) * gradient * gradient
    first_hat = first_new / (1.0 - beta_one ** step_count)
    second_hat = second_new / (1.0 - beta_two ** step_count)
    weight_new = weight - learn_rate * (first_hat / (jnp.sqrt(second_hat) + adam_eps) + weight_decay * weight)
    return (weight_new, first_new, second_new)

def rotate(values, positions):
    half = values.shape[-1] // 2
    freq = rope_theta ** (-jnp.arange(half, dtype=jnp.float32) * 2.0 / values.shape[-1])
    angle = positions.astype(jnp.float32)[..., None] * freq
    cosine = jnp.cos(angle)
    sine = jnp.sin(angle)
    first_half = values[..., :half]
    second_half = values[..., half:]
    return jnp.concatenate([first_half * cosine - second_half * sine, second_half * cosine + first_half * sine], axis=-1)

def project_keys(hidden_size, quantized_weight, scales, lengths):
    decode_step_count, row_count, block_width = hidden_size.shape
    block_count = scales.shape[0]
    part_count = jnp.einsum('qht,hti->qhi', hidden_size.reshape(decode_step_count * row_count, block_count, block_width // block_count).astype(jnp.float32), quantized_weight.reshape(block_count, block_width // block_count, -1).astype(jnp.float32))
    raw = lax.optimization_barrier(jnp.sum(part_count * scales[None, :, None], axis=1)).reshape(decode_step_count, row_count, -1)
    positions = lengths[None, :] + jnp.arange(decode_step_count, dtype=jnp.int32)[:, None]
    return rotate(raw, positions).astype(jnp.bfloat16)

def attend(query, cache_keys, cache_values, fresh, fresh_values, lengths):
    decode_step_count, row_count, joined = query.shape
    head_dim = cache_keys.shape[-1]
    heads = joined // head_dim
    keys_c = cache_keys.astype(jnp.float32)
    values_c = cache_values.astype(jnp.float32)
    keys_f = fresh.astype(jnp.float32)
    values_f = fresh_values.astype(jnp.float32)
    valid = jnp.arange(cache_keys.shape[1], dtype=jnp.int32)[None, None, :] < lengths[:, None, None]
    outputs = []
    for section_index in range(decode_step_count):
        query_now = query[section_index].reshape(row_count, heads, head_dim).astype(jnp.float32)
        scores_c = jnp.einsum('rhd,rcd->rhc', query_now, keys_c) / math.sqrt(head_dim)
        scores_f = jnp.einsum('rhd,trd->rht', query_now, keys_f) / math.sqrt(head_dim)
        scores_c = jnp.where(valid, scores_c, -jnp.inf)
        scores_f = jnp.where((jnp.arange(decode_step_count) <= section_index)[None, None, :], scores_f, -jnp.inf)
        peak = jnp.maximum(lax.optimization_barrier(jnp.max(scores_c, axis=2)), lax.optimization_barrier(jnp.max(scores_f, axis=2)))[:, :, None]
        exp_c = jnp.exp(scores_c - peak)
        exp_f = jnp.exp(scores_f - peak)
        total = lax.optimization_barrier(jnp.sum(exp_c, axis=2, keepdims=True)) + lax.optimization_barrier(jnp.sum(exp_f, axis=2, keepdims=True))
        prob_c = (exp_c / total).astype(jnp.bfloat16)
        prob_f = (exp_f / total).astype(jnp.bfloat16)
        mixed = jnp.einsum('rhc,rcd->rhd', prob_c.astype(jnp.float32), values_c)
        mixed = mixed + jnp.einsum('rht,trd->rhd', prob_f.astype(jnp.float32), values_f)
        outputs.append(mixed.reshape(row_count, joined).astype(jnp.bfloat16))
    return jnp.stack(outputs)

def reference(tokens_x, cotangent, master_weight, first_moment, second_moment, hidden_dec, queries, new_values, key_cache, value_cache, cache_lengths):
    gradient = lax.dot_general(tokens_x, cotangent, (((0,), (0,)), ((), ())), preferred_element_type=jnp.float32)
    weight_next, first_next, second_next = adamw(master_weight, first_moment, second_moment, gradient)
    blocks = weight_next.reshape(D // BLOCK, BLOCK, HD)
    scales = lax.optimization_barrier(jnp.max(jnp.abs(blocks), axis=(1, 2))) + peak_eps
    rollout_weight = (blocks / scales[:, None, None]).reshape(D, HD).astype(jnp.bfloat16)
    fresh_keys = project_keys(hidden_dec, rollout_weight, scales, cache_lengths)
    group_rows = 32
    groups = ROWS // group_rows

    def by_rows(array):
        return array.reshape((array.shape[0], groups, group_rows) + array.shape[2:]).swapaxes(0, 1)
    packed = (by_rows(queries), key_cache.reshape(groups, group_rows, CACHE, HD), value_cache.reshape(groups, group_rows, CACHE, HD), by_rows(fresh_keys), by_rows(new_values), cache_lengths.reshape(groups, group_rows))
    mapped = lax.map(lambda items: attend(*items), packed)
    attended = mapped.swapaxes(0, 1).reshape(STEPS, ROWS, QPK * HD)
    return (weight_next, first_next, second_next, rollout_weight, fresh_keys, attended)
```

```python
import functools
import math

import jax
import jax.numpy as jnp
from jax import lax
from jax.experimental import pallas as pl
from jax.experimental.pallas import tpu as pltpu
from jax.sharding import PartitionSpec as P

D = 8192
BLOCK = 128


beta_one = 0.9
beta_two = 0.95
adam_eps = 1e-08
learn_rate = 0.0003
weight_decay = 0.1
step_count = 100
rope_theta = 1000000.0
peak_eps = 1e-06


def adamw(weight, first, second, gradient):
    first_new = beta_one * first + (1.0 - beta_one) * gradient
    second_new = beta_two * second + (1.0 - beta_two) * gradient * gradient
    first_hat = first_new / (1.0 - beta_one**step_count)
    second_hat = second_new / (1.0 - beta_two**step_count)
    weight_new = weight - learn_rate * (
        first_hat / (jnp.sqrt(second_hat) + adam_eps) + weight_decay * weight
    )
    return (weight_new, first_new, second_new)


def rotate(values, positions):
    half = values.shape[-1] // 2
    freq = rope_theta ** (-jnp.arange(half, dtype=jnp.float32) * 2.0 / values.shape[-1])
    angle = positions.astype(jnp.float32)[..., None] * freq
    cosine = jnp.cos(angle)
    sine = jnp.sin(angle)
    first_half = values[..., :half]
    second_half = values[..., half:]
    return jnp.concatenate(
        [first_half * cosine - second_half * sine, second_half * cosine + first_half * sine],
        axis=-1,
    )


def project_keys(hidden_size, quantized_weight, scales, lengths):
    decode_step_count, row_count, block_width = hidden_size.shape
    block_count = scales.shape[0]
    part_count = jnp.einsum(
        "qht,hti->qhi",
        hidden_size.reshape(decode_step_count * row_count, block_count, block_width // block_count),
        quantized_weight.reshape(block_count, block_width // block_count, -1),
        preferred_element_type=jnp.float32,
    )
    raw = jnp.sum(part_count * scales[None, :, None], axis=1).reshape(
        decode_step_count, row_count, -1
    )
    positions = lengths[None, :] + jnp.arange(decode_step_count, dtype=jnp.int32)[:, None]
    return rotate(raw, positions).astype(jnp.bfloat16)


def attend(query, cache_keys, cache_values, fresh, fresh_values, lengths):
    decode_step_count, row_count, joined = query.shape
    head_dim = cache_keys.shape[-1]
    heads = joined // head_dim
    valid = jnp.arange(cache_keys.shape[1], dtype=jnp.int32)[None, None, :] < lengths[:, None, None]
    outputs = []
    for section_index in range(decode_step_count):
        query_now = query[section_index].reshape(row_count, heads, head_dim)
        scores_c = jnp.einsum(
            "rhd,rcd->rhc", query_now, cache_keys, preferred_element_type=jnp.float32
        ) / math.sqrt(head_dim)
        scores_f = jnp.einsum(
            "rhd,trd->rht", query_now, fresh, preferred_element_type=jnp.float32
        ) / math.sqrt(head_dim)
        scores_c = jnp.where(valid, scores_c, -jnp.inf)
        scores_f = jnp.where(
            (jnp.arange(decode_step_count) <= section_index)[None, None, :], scores_f, -jnp.inf
        )
        peak = jnp.maximum(jnp.max(scores_c, axis=2), jnp.max(scores_f, axis=2))[:, :, None]
        exp_c = jnp.exp(scores_c - peak)
        exp_f = jnp.exp(scores_f - peak)
        total = jnp.sum(exp_c, axis=2, keepdims=True) + jnp.sum(exp_f, axis=2, keepdims=True)
        prob_c = (exp_c / total).astype(jnp.bfloat16)
        prob_f = (exp_f / total).astype(jnp.bfloat16)
        mixed = jnp.einsum("rhc,rcd->rhd", prob_c, cache_values, preferred_element_type=jnp.float32)
        mixed = mixed + jnp.einsum(
            "rht,trd->rhd", prob_f, fresh_values, preferred_element_type=jnp.float32
        )
        outputs.append(mixed.reshape(row_count, joined).astype(jnp.bfloat16))
    return jnp.stack(outputs)


def shards(
    tokens_x,
    cotangent,
    master_weight,
    first_moment,
    second_moment,
    hidden_dec,
    queries,
    new_values,
    key_cache,
    value_cache,
    cache_lengths,
):
    shard_rows = master_weight.shape[0]
    partial_grad = lax.psum_scatter(
        lax.dot_general(
            tokens_x, cotangent, (((0,), (0,)), ((), ())), preferred_element_type=jnp.float32
        ),
        "fsdp",
        scatter_dimension=0,
        tiled=True,
    )
    gradient = lax.psum(partial_grad, "rep")
    weight_next, first_next, second_next = adamw(
        master_weight, first_moment, second_moment, gradient
    )
    block_count = D // BLOCK
    row_ids = lax.axis_index("fsdp") * shard_rows + jnp.arange(shard_rows, dtype=jnp.int32)
    member = (row_ids // BLOCK)[:, None] == jnp.arange(block_count, dtype=jnp.int32)[None, :]
    row_peak = jnp.max(jnp.abs(weight_next), axis=1)
    local_peaks = jnp.max(jnp.where(member, row_peak[:, None], 0.0), axis=0)
    scales = lax.pmax(local_peaks, "fsdp") + peak_eps
    row_scale = jnp.sum(jnp.where(member, scales[None, :], 0.0), axis=1)
    local_quant = (weight_next / row_scale[:, None]).astype(jnp.bfloat16)
    rollout_weight = lax.all_gather(local_quant, "fsdp", axis=0, tiled=True)
    fresh_keys = project_keys(hidden_dec, rollout_weight, scales, cache_lengths)
    attended = attend(queries, key_cache, value_cache, fresh_keys, new_values, cache_lengths)
    return (weight_next, first_next, second_next, rollout_weight, fresh_keys, attended)


MESH = pl.DeviceIdType.MESH
F32 = jnp.float32
BF16 = jnp.bfloat16
TAIL = 16


def tdot(a, b):
    return lax.dot_general(a, b, (((0,), (0,)), ((), ())), preferred_element_type=F32)


def step_kernel(
    nz, tok, cot, wt, mo, ve, hid, qr, nv, kc, vc, lens, cosr, sinr,
    w_o, m_o, v_o, roll_o, fk_o, att_o,
    sib, sibcot, rs_s, rs_r, keep_b, keep_own, z_s, z_r, g_q, ag, qs, ex, mx, sm,
    sib_ss, sib_rs, rs_ss, rs_rs, z_ss, z_rs, g_ss, g_rs,
    az_ss, az_rs, ap_ss, ap_rs, as_ss, as_rs, o_s,
):
    f = lax.axis_index("fsdp")
    r = lax.axis_index("rep")
    z, x = lax.div(f, 2), lax.rem(f, 2)
    y, c = lax.div(r, 2), lax.rem(r, 2)
    shard = wt.shape[0]
    half = shard // 2
    quarter = shard // 4
    blocks = quarter // BLOCK
    steps, rows, joined = qr.shape
    hd = kc.shape[2]
    heads = joined // hd

    def flip(value, bit):
        return 1 - value if bit else value

    def device(dz=0, dx=0, dy=0, dc=0):
        zz = lax.rem(z + dz, nz) if dz else z
        return {"fsdp": zz * 2 + flip(x, dx), "rep": flip(y, dy) * 2 + flip(c, dc)}

    def remote(src, dst, ss, rs, where):
        return pltpu.make_async_remote_copy(
            src_ref=src, dst_ref=dst, send_sem=ss, recv_sem=rs,
            device_id=where, device_id_type=MESH,
        )

    sibling = device(dc=1)
    xn, yn = device(dx=1), device(dy=1)
    zpeer = [device(dz=1 + j) for j in range(nz - 1)]
    barrier = pltpu.get_barrier_semaphore()
    peers = [sibling, xn, yn] + zpeer
    for peer in peers:
        pl.semaphore_signal(barrier, inc=1, device_id=peer, device_id_type=MESH)

    scale = 1.0 / math.sqrt(hd)
    for i in range(rows):
        for s in range(steps):
            for h in range(heads):
                qs[i, s * heads + h : s * heads + h + 1, :] = qr[
                    s, i : i + 1, h * hd : (h + 1) * hd
                ].astype(F32)
    for i in range(rows):
        sc = lax.dot_general(
            qs[i].astype(BF16), kc[i], (((1,), (1,)), ((), ())), preferred_element_type=F32
        ) * scale
        slot = lax.broadcasted_iota(jnp.int32, sc.shape, 1)
        sc = jnp.where(slot < lens[i], sc, -jnp.inf)
        top = jnp.max(sc, axis=1, keepdims=True)
        e = jnp.exp(sc - top)
        ex[i] = e
        mx[i] = jnp.broadcast_to(top, mx.shape[1:])
        sm[i] = jnp.broadcast_to(jnp.sum(e, axis=1, keepdims=True), sm.shape[1:])

    pl.semaphore_wait(barrier, len(peers))

    def target(j):
        return lax.rem(z + 1 + j, nz)

    sends = []

    def go(copy):
        copy.start()
        sends.append(copy)
        return copy

    cot_in = go(remote(cot, sibcot, sib_ss.at[2 * nz], sib_rs.at[2 * nz], sibling))
    sib_in = {}
    for j in range(nz):
        for dx in (1, 0):
            k = 2 * j + dx
            off = pl.multiple_of((target(j) * 2 + flip(x, dx)) * shard + (1 - c) * half, BLOCK)
            sib_in[j, dx] = go(
                remote(tok.at[:, pl.ds(off, half)], sib.at[k], sib_ss.at[k], sib_rs.at[k], sibling)
            )
    cot_in.wait_recv()

    def part(j, dx, dy):
        at = flip(y, dy) * quarter
        off = pl.multiple_of((target(j) * 2 + flip(x, dx)) * shard + c * half + at, BLOCK)
        at = pl.multiple_of(at, BLOCK)
        return tdot(tok[:, pl.ds(off, quarter)], cot[...]) + tdot(
            sib[2 * j + dx, :, pl.ds(at, quarter)], sibcot[...]
        )

    def first(j):
        return (1, 0) if j % 2 == 0 else (0, 1)

    rs_in = {}

    def stage_a(j):
        da = first(j)
        near, far = (xn, yn) if j % 2 == 0 else (yn, xn)
        sib_in[j, 1].wait_recv()
        if j % 2:
            sib_in[j, 0].wait_recv()
        rs_s[1, j] = part(j, 1, 1).astype(BF16)
        rs_in[1, j] = go(remote(rs_s.at[1, j], rs_r.at[1, j], rs_ss.at[1, j], rs_rs.at[1, j], near))
        rs_s[0, j] = part(j, *da).astype(BF16)
        rs_in[0, j] = go(remote(rs_s.at[0, j], rs_r.at[0, j], rs_ss.at[0, j], rs_rs.at[0, j], near))
        if j % 2 == 0:
            sib_in[j, 0].wait_recv()
        keep_b[j] = part(j, da[1], da[0])
        keep_own[j] = part(j, 0, 0)

    def stage_b(j):
        far = yn if j % 2 == 0 else xn
        rs_in[1, j].wait_recv()
        rs_s[2, j] = (keep_b[j] + rs_r[1, j].astype(F32)).astype(BF16)
        rs_in[2, j] = go(remote(rs_s.at[2, j], rs_r.at[2, j], rs_ss.at[2, j], rs_rs.at[2, j], far))

    z_in = {}

    def stage_z(j):
        rs_in[0, j].wait_recv()
        rs_in[2, j].wait_recv()
        total = keep_own[j] + rs_r[0, j].astype(F32) + rs_r[2, j].astype(F32)
        if j == nz - 1:
            return total
        z_s[j] = total.astype(BF16)
        z_in[j] = go(remote(z_s.at[j], z_r.at[j], z_ss.at[j], z_rs.at[j], zpeer[j]))
        return None

    for j in range(nz):
        stage_a(j)
    stage_b(0)
    for j in range(1, nz):
        stage_b(j)
        stage_z(j - 1)
    grad = stage_z(nz - 1)
    for j in range(nz - 1):
        z_in[j].wait_recv()
        grad = grad + z_r[j].astype(F32)
    g_q[0] = grad
    g_in = {
        2: go(remote(g_q.at[0], g_q.at[2], g_ss.at[2], g_rs.at[2], sibling)),
    }

    def update(gradient, dy, dc):
        at = pl.ds(pl.multiple_of((flip(c, dc) * 2 + flip(y, dy)) * quarter, BLOCK), quarter)
        new = adamw(wt[at, :], mo[at, :], ve[at, :], gradient)
        w_o[at, :], m_o[at, :], v_o[at, :] = new
        return new[0]

    fresh = update(grad, 0, 0)
    row = lax.broadcasted_iota(jnp.int32, (TAIL, hd), 0)
    tail = jnp.zeros((TAIL, hd), F32)
    for b in range(blocks):
        piece = fresh[b * BLOCK : (b + 1) * BLOCK]
        peak = jnp.max(jnp.max(jnp.abs(piece), axis=0, keepdims=True), axis=1, keepdims=True)
        peak = peak + peak_eps
        ag[0, 0, nz - 1, b * BLOCK : (b + 1) * BLOCK] = (piece / peak).astype(BF16)
        rest = jnp.broadcast_to(peak, (TAIL, hd))
        for k in range(3):
            high = rest.astype(BF16).astype(F32)
            tail = jnp.where(row == 3 * b + k, high, tail)
            rest = rest - high
    ag[0, 0, nz - 1, quarter : quarter + TAIL] = tail.astype(BF16)

    az_in = {
        j: go(remote(ag.at[0, 0, nz - 1], ag.at[0, 0, j], az_ss.at[j], az_rs.at[j], zpeer[j]))
        for j in range(nz - 1)
    }
    outs = []
    raw = [jnp.zeros((steps * rows, hd), F32)]
    ap_in, as_in = {}, {}

    def place(dc, p, j):
        shard_at = lax.rem(z + nz - 1 - j, nz) * 2 + flip(x, p & 1)
        return shard_at * shard + (flip(c, dc) * 2 + flip(y, p >> 1)) * quarter

    def emit(dc, p, j):
        n = (dc * 4 + p) * nz + j
        copy = pltpu.make_async_copy(
            ag.at[dc, p, j, pl.ds(0, quarter)],
            roll_o.at[pl.ds(pl.multiple_of(place(dc, p, j), BLOCK), quarter)],
            o_s.at[n],
        )
        copy.start()
        outs.append(copy)

    def project(dc, p, j):
        at = place(dc, p, j)
        t = ag[dc, p, j, quarter : quarter + TAIL].astype(F32)
        for b in range(blocks):
            peak = t[3 * b : 3 * b + 1] + t[3 * b + 1 : 3 * b + 2] + t[3 * b + 2 : 3 * b + 3]
            h = hid[:, pl.ds(pl.multiple_of(at + b * BLOCK, BLOCK), BLOCK)]
            got = jnp.dot(
                h, ag[dc, p, j, b * BLOCK : (b + 1) * BLOCK], preferred_element_type=F32
            )
            raw[0] = raw[0] + got * peak

    def share(p, j):
        as_in[p, j] = go(
            remote(ag.at[0, p, j], ag.at[1, p, j], as_ss.at[p, j], as_rs.at[p, j], sibling)
        )

    def plane(src, p, j, where):
        ap_in[p, j] = go(
            remote(ag.at[0, src, j], ag.at[0, p, j], ap_ss.at[p - 1, j], ap_rs.at[p - 1, j], where)
        )

    def spread(j):
        if j < nz - 1:
            az_in[j].wait_recv()
        plane(0, 1, j, xn)
        plane(0, 2, j, yn)
        share(0, j)
        emit(0, 0, j)
        project(0, 0, j)

    def relay(j):
        ap_in[1, j].wait_recv()
        if j % 2 == 0:
            plane(1, 3, j, yn)
        share(1, j)
        ap_in[2, j].wait_recv()
        if j % 2 == 1:
            plane(2, 3, j, xn)
        share(2, j)
        emit(0, 1, j)
        emit(0, 2, j)
        project(0, 1, j)
        project(0, 2, j)

    def last(j):
        ap_in[3, j].wait_recv()
        share(3, j)
        emit(0, 3, j)
        project(0, 3, j)

    def cross(p, j):
        as_in[p, j].wait_recv()
        emit(1, p, j)
        project(1, p, j)

    spread(nz - 1)
    g_in[1] = go(remote(g_q.at[0], g_q.at[1], g_ss.at[1], g_rs.at[1], yn))
    g_in[2].wait_recv()
    update(g_q[2], 0, 1)
    order = [nz - 1] + list(range(nz - 1))
    for i in range(1, nz):
        spread(order[i])
        relay(order[i - 1])
        cross(0, order[i - 1])
    g_in[1].wait_recv()
    g_in[3] = go(remote(g_q.at[1], g_q.at[3], g_ss.at[3], g_rs.at[3], sibling))
    update(g_q[1], 1, 0)
    relay(order[-1])
    g_in[3].wait_recv()
    update(g_q[3], 1, 1)
    for j in order:
        last(j)
    cross(0, order[-1])
    for p in (1, 2, 3):
        for j in order:
            cross(p, j)

    keys = raw[0] * cosr[...] + pltpu.roll(raw[0], hd // 2, 1) * sinr[...]
    keys = keys.astype(BF16)
    for s in range(steps):
        fk_o[s] = keys[s * rows : (s + 1) * rows]
    keys = keys.astype(F32)
    step_of = lax.broadcasted_iota(jnp.int32, (steps * heads, 1), 0) // heads
    lines = [[] for _ in range(steps)]
    for i in range(rows):
        query = qs[i]
        top_c = mx[i][:, :1]
        sum_c = sm[i][:, :1]
        top = top_c
        scf = []
        for t in range(steps):
            k = keys[t * rows + i : t * rows + i + 1]
            sc = jnp.sum(query * k, axis=1, keepdims=True) * scale
            sc = jnp.where(step_of >= t, sc, -jnp.inf)
            scf.append(sc)
            top = jnp.maximum(top, sc)
        exf = [jnp.exp(sc - top) for sc in scf]
        fix = jnp.exp(top_c - top)
        total = sum_c * fix
        for e in exf:
            total = total + e
        prob = (ex[i] * (fix / total)).astype(BF16)
        mixed = jnp.dot(prob, vc[i], preferred_element_type=F32)
        for t in range(steps):
            pf = (exf[t] / total).astype(BF16).astype(F32)
            mixed = mixed + pf * nv[t, i : i + 1, :].astype(F32)
        for s in range(steps):
            lines[s].append(
                jnp.concatenate(
                    [mixed[s * heads + h : s * heads + h + 1] for h in range(heads)], axis=1
                )
            )
    for s in range(steps):
        att_o[s] = jnp.concatenate(lines[s], axis=0).astype(BF16)
    for copy in sends:
        copy.wait_send()
    for copy in outs:
        copy.wait()


def fused(
    nz, tokens_x, cotangent, master_weight, first_moment, second_moment,
    hidden_dec, queries, new_values, key_cache, value_cache, cache_lengths,
):
    steps, rows, width = hidden_dec.shape
    shard, hd = master_weight.shape
    quarter = shard // 4
    slots = key_cache.shape[1]
    qrows = queries.shape[2] // hd * steps
    tokens = tokens_x.shape[0]
    half = hd // 2
    freq = rope_theta ** (-jnp.arange(half, dtype=F32) * 2.0 / hd)
    positions = cache_lengths[None, :] + jnp.arange(steps, dtype=jnp.int32)[:, None]
    angle = positions.astype(F32).reshape(-1, 1) * freq
    cosine, sine = jnp.cos(angle), jnp.sin(angle)
    cosr = jnp.concatenate([cosine, cosine], axis=1)
    sinr = jnp.concatenate([-sine, sine], axis=1)
    vm = pl.BlockSpec(memory_space=pltpu.VMEM)
    dma = pltpu.SemaphoreType.DMA
    shape = jax.ShapeDtypeStruct
    return pl.pallas_call(
        functools.partial(step_kernel, nz),
        out_shape=(
            shape((shard, hd), F32), shape((shard, hd), F32), shape((shard, hd), F32),
            shape((width, hd), BF16), shape(new_values.shape, BF16), shape(queries.shape, BF16),
        ),
        in_specs=[vm] * 10 + [pl.BlockSpec(memory_space=pltpu.SMEM)] + [vm] * 2,
        out_specs=(vm, vm, vm, pl.BlockSpec(memory_space=pl.ANY), vm, vm),
        scratch_shapes=[
            pltpu.VMEM((2 * nz, tokens, shard // 2), BF16),
            pltpu.VMEM((tokens, hd), BF16),
            pltpu.VMEM((3, nz, quarter, hd), BF16),
            pltpu.VMEM((3, nz, quarter, hd), BF16),
            pltpu.VMEM((nz, quarter, hd), F32),
            pltpu.VMEM((nz, quarter, hd), F32),
            pltpu.VMEM((nz - 1, quarter, hd), BF16),
            pltpu.VMEM((nz - 1, quarter, hd), BF16),
            pltpu.VMEM((4, quarter, hd), F32),
            pltpu.VMEM((2, 4, nz, quarter + TAIL, hd), BF16),
            pltpu.VMEM((rows, qrows, hd), F32),
            pltpu.VMEM((rows, qrows, slots), F32),
            pltpu.VMEM((rows, qrows, hd), F32),
            pltpu.VMEM((rows, qrows, hd), F32),
            dma((2 * nz + 1,)), dma((2 * nz + 1,)),
            dma((3, nz)), dma((3, nz)),
            dma((nz - 1,)), dma((nz - 1,)),
            dma((4,)), dma((4,)),
            dma((nz - 1,)), dma((nz - 1,)),
            dma((3, nz)), dma((3, nz)),
            dma((4, nz)), dma((4, nz)),
            dma((8 * nz,)),
        ],
        compiler_params=pltpu.CompilerParams(
            collective_id=0, has_side_effects=True, vmem_limit_bytes=40 * 1024 * 1024
        ),
        name="step",
    )(
        tokens_x, cotangent, master_weight, first_moment, second_moment,
        hidden_dec.reshape(steps * rows, width), queries, new_values,
        key_cache, value_cache, cache_lengths, cosr, sinr,
    )


def body(parts, replicas, *args):
    quarter, left = divmod(args[2].shape[0], 4)
    fits = replicas == 4 and parts >= 4 and parts % 2 == 0 and left == 0 and quarter % BLOCK == 0
    if fits and quarter // BLOCK * 3 <= TAIL:
        return fused(parts // 2, *args)
    return shards(*args)


def solution(mesh):
    return jax.shard_map(
        functools.partial(body, mesh.shape["fsdp"], mesh.shape["rep"]),
        mesh=mesh,
        in_specs=(
            P(("fsdp", "rep"), None),
            P(("fsdp", "rep"), None),
            P("fsdp", None),
            P("fsdp", None),
            P("fsdp", None),
            P(None, ("fsdp", "rep"), None),
            P(None, ("fsdp", "rep"), None),
            P(None, ("fsdp", "rep"), None),
            P(("fsdp", "rep"), None, None),
            P(("fsdp", "rep"), None, None),
            P(("fsdp", "rep")),
        ),
        out_specs=(
            P("fsdp", None),
            P("fsdp", None),
            P("fsdp", None),
            P(),
            P(None, ("fsdp", "rep"), None),
            P(None, ("fsdp", "rep"), None),
        ),
        check_vma=False,
    )
```

```python
import functools
import math

import jax
import jax.numpy as jnp
from jax import lax
from jax.experimental import pallas as pl
from jax.experimental.pallas import tpu as pltpu
from jax.sharding import PartitionSpec as P

D = 8192
BLOCK = 128


beta_one = 0.9
beta_two = 0.95
adam_eps = 1e-08
learn_rate = 0.0003
weight_decay = 0.1
step_count = 100
rope_theta = 1000000.0
peak_eps = 1e-06


def adamw(weight, first, second, gradient):
    first_new = beta_one * first + (1.0 - beta_one) * gradient
    second_new = beta_two * second + (1.0 - beta_two) * gradient * gradient
    first_hat = first_new / (1.0 - beta_one**step_count)
    second_hat = second_new / (1.0 - beta_two**step_count)
    weight_new = weight - learn_rate * (
        first_hat / (jnp.sqrt(second_hat) + adam_eps) + weight_decay * weight
    )
    return (weight_new, first_new, second_new)


def rotate(values, positions):
    half = values.shape[-1] // 2
    freq = rope_theta ** (-jnp.arange(half, dtype=jnp.float32) * 2.0 / values.shape[-1])
    angle = positions.astype(jnp.float32)[..., None] * freq
    cosine = jnp.cos(angle)
    sine = jnp.sin(angle)
    first_half = values[..., :half]
    second_half = values[..., half:]
    return jnp.concatenate(
        [first_half * cosine - second_half * sine, second_half * cosine + first_half * sine],
        axis=-1,
    )


def project_keys(hidden_size, quantized_weight, scales, lengths):
    decode_step_count, row_count, block_width = hidden_size.shape
    block_count = scales.shape[0]
    part_count = jnp.einsum(
        "qht,hti->qhi",
        hidden_size.reshape(decode_step_count * row_count, block_count, block_width // block_count),
        quantized_weight.reshape(block_count, block_width // block_count, -1),
        preferred_element_type=jnp.float32,
    )
    raw = jnp.sum(part_count * scales[None, :, None], axis=1).reshape(
        decode_step_count, row_count, -1
    )
    positions = lengths[None, :] + jnp.arange(decode_step_count, dtype=jnp.int32)[:, None]
    return rotate(raw, positions).astype(jnp.bfloat16)


def attend(query, cache_keys, cache_values, fresh, fresh_values, lengths):
    decode_step_count, row_count, joined = query.shape
    head_dim = cache_keys.shape[-1]
    heads = joined // head_dim
    valid = jnp.arange(cache_keys.shape[1], dtype=jnp.int32)[None, None, :] < lengths[:, None, None]
    outputs = []
    for section_index in range(decode_step_count):
        query_now = query[section_index].reshape(row_count, heads, head_dim)
        scores_c = jnp.einsum(
            "rhd,rcd->rhc", query_now, cache_keys, preferred_element_type=jnp.float32
        ) / math.sqrt(head_dim)
        scores_f = jnp.einsum(
            "rhd,trd->rht", query_now, fresh, preferred_element_type=jnp.float32
        ) / math.sqrt(head_dim)
        scores_c = jnp.where(valid, scores_c, -jnp.inf)
        scores_f = jnp.where(
            (jnp.arange(decode_step_count) <= section_index)[None, None, :], scores_f, -jnp.inf
        )
        peak = jnp.maximum(jnp.max(scores_c, axis=2), jnp.max(scores_f, axis=2))[:, :, None]
        exp_c = jnp.exp(scores_c - peak)
        exp_f = jnp.exp(scores_f - peak)
        total = jnp.sum(exp_c, axis=2, keepdims=True) + jnp.sum(exp_f, axis=2, keepdims=True)
        prob_c = (exp_c / total).astype(jnp.bfloat16)
        prob_f = (exp_f / total).astype(jnp.bfloat16)
        mixed = jnp.einsum("rhc,rcd->rhd", prob_c, cache_values, preferred_element_type=jnp.float32)
        mixed = mixed + jnp.einsum(
            "rht,trd->rhd", prob_f, fresh_values, preferred_element_type=jnp.float32
        )
        outputs.append(mixed.reshape(row_count, joined).astype(jnp.bfloat16))
    return jnp.stack(outputs)


def shards(
    tokens_x,
    cotangent,
    master_weight,
    first_moment,
    second_moment,
    hidden_dec,
    queries,
    new_values,
    key_cache,
    value_cache,
    cache_lengths,
):
    shard_rows = master_weight.shape[0]
    partial_grad = lax.psum_scatter(
        lax.dot_general(
            tokens_x, cotangent, (((0,), (0,)), ((), ())), preferred_element_type=jnp.float32
        ),
        "fsdp",
        scatter_dimension=0,
        tiled=True,
    )
    gradient = lax.psum(partial_grad, "rep")
    weight_next, first_next, second_next = adamw(
        master_weight, first_moment, second_moment, gradient
    )
    block_count = D // BLOCK
    row_ids = lax.axis_index("fsdp") * shard_rows + jnp.arange(shard_rows, dtype=jnp.int32)
    member = (row_ids // BLOCK)[:, None] == jnp.arange(block_count, dtype=jnp.int32)[None, :]
    row_peak = jnp.max(jnp.abs(weight_next), axis=1)
    local_peaks = jnp.max(jnp.where(member, row_peak[:, None], 0.0), axis=0)
    scales = lax.pmax(local_peaks, "fsdp") + peak_eps
    row_scale = jnp.sum(jnp.where(member, scales[None, :], 0.0), axis=1)
    local_quant = (weight_next / row_scale[:, None]).astype(jnp.bfloat16)
    rollout_weight = lax.all_gather(local_quant, "fsdp", axis=0, tiled=True)
    fresh_keys = project_keys(hidden_dec, rollout_weight, scales, cache_lengths)
    attended = attend(queries, key_cache, value_cache, fresh_keys, new_values, cache_lengths)
    return (weight_next, first_next, second_next, rollout_weight, fresh_keys, attended)


MESH = pl.DeviceIdType.MESH
F32 = jnp.float32
BF16 = jnp.bfloat16
TAIL = 16


def tdot(a, b):
    return lax.dot_general(a, b, (((0,), (0,)), ((), ())), preferred_element_type=F32)


def step_kernel(
    nz, tok_h, cot_h, wt_h, mo_h, ve_h, hid_h, qr_h, nv_h, kc_h, vc_h, lens_h,
    w_o, m_o, v_o, ag, raw_o, qs, ex, mx, sm, vc, nv,
    tok, cot, wt, mo, ve, hid3, hid, qr, kc, lens, in_s,
    sib, sibcot, rs_s, rs_r, keep_b, keep_own, z_s, z_r, g_q,
    sib_ss, sib_rs, rs_ss, rs_rs, z_ss, z_rs, g_ss, g_rs,
    az_ss, az_rs, ap_ss, ap_rs, as_ss, as_rs,
):
    f = lax.axis_index("fsdp")
    r = lax.axis_index("rep")
    z, x = lax.div(f, 2), lax.rem(f, 2)
    y, c = lax.div(r, 2), lax.rem(r, 2)
    shard = wt.shape[0]
    half = shard // 2
    quarter = shard // 4
    blocks = quarter // BLOCK
    steps, rows, joined = qr.shape
    hd = kc.shape[2]
    heads = joined // hd

    def flip(value, bit):
        return 1 - value if bit else value

    def device(dz=0, dx=0, dy=0, dc=0):
        zz = lax.rem(z + dz, nz) if dz else z
        return {"fsdp": zz * 2 + flip(x, dx), "rep": flip(y, dy) * 2 + flip(c, dc)}

    def remote(src, dst, ss, rs, where):
        return pltpu.make_async_remote_copy(
            src_ref=src, dst_ref=dst, send_sem=ss, recv_sem=rs,
            device_id=where, device_id_type=MESH,
        )

    sibling = device(dc=1)
    xn, yn = device(dx=1), device(dy=1)
    zpeer = [device(dz=1 + j) for j in range(nz - 1)]
    barrier = pltpu.get_barrier_semaphore()
    peers = [sibling, xn, yn] + zpeer
    for peer in peers:
        pl.semaphore_signal(barrier, inc=1, device_id=peer, device_id_type=MESH)

    loads = [
        pltpu.make_async_copy(a, b, in_s.at[n])
        for n, (a, b) in enumerate((
            (tok_h, tok), (cot_h, cot), (qr_h, qr), (kc_h, kc), (lens_h, lens), (hid_h, hid3),
            (wt_h, wt), (mo_h, mo), (ve_h, ve), (vc_h, vc), (nv_h, nv),
        ))
    ]
    for load in loads:
        load.start()
    for load in loads[2:6]:
        load.wait()
    hid[...] = jnp.concatenate([hid3[s].astype(F32) for s in range(steps)], axis=0).astype(BF16)

    scale = 1.0 / math.sqrt(hd)
    for i in range(rows):
        for s in range(steps):
            for h in range(heads):
                qs[i, s * heads + h : s * heads + h + 1, :] = qr[
                    s, i : i + 1, h * hd : (h + 1) * hd
                ].astype(F32)
    for i in range(rows):
        sc = lax.dot_general(
            qs[i].astype(BF16), kc[i], (((1,), (1,)), ((), ())), preferred_element_type=F32
        ) * scale
        slot = lax.broadcasted_iota(jnp.int32, sc.shape, 1)
        sc = jnp.where(slot < lens[i], sc, -jnp.inf)
        top = jnp.max(sc, axis=1, keepdims=True)
        e = jnp.exp(sc - top)
        ex[i] = e
        mx[i] = jnp.broadcast_to(top, mx.shape[1:])
        sm[i] = jnp.broadcast_to(jnp.sum(e, axis=1, keepdims=True), sm.shape[1:])

    row = lax.broadcasted_iota(jnp.int32, (steps * rows, hd), 0)
    lane = lax.broadcasted_iota(jnp.int32, (steps * rows, hd), 1)
    position = row // rows
    for i in range(rows):
        position = position + jnp.where(row % rows == i, lens[i], 0)
    freq = jnp.exp((lane % (hd // 2)).astype(F32) * (-2.0 * math.log(rope_theta) / hd))
    angle = position.astype(F32) * freq
    cosr = jnp.cos(angle)
    sine = jnp.sin(angle)
    sinr = jnp.where(lane < hd // 2, -sine, sine)

    pl.semaphore_wait(barrier, len(peers))

    def target(j):
        return lax.rem(z + 1 + j, nz)

    sends = []

    def go(copy):
        copy.start()
        sends.append(copy)
        return copy

    cot_in = go(remote(cot_h, sibcot, sib_ss.at[2 * nz], sib_rs.at[2 * nz], sibling))
    sib_in = {}
    for j in range(nz):
        for dx in (1, 0):
            k = 2 * j + dx
            off = pl.multiple_of((target(j) * 2 + flip(x, dx)) * shard + (1 - c) * half, BLOCK)
            sib_in[j, dx] = go(
                remote(tok_h.at[:, pl.ds(off, half)], sib.at[k], sib_ss.at[k], sib_rs.at[k], sibling)
            )
    cot_in.wait_recv()
    loads[0].wait()
    loads[1].wait()

    def part(j, dx, dy):
        at = flip(y, dy) * quarter
        off = pl.multiple_of((target(j) * 2 + flip(x, dx)) * shard + c * half + at, BLOCK)
        at = pl.multiple_of(at, BLOCK)
        return tdot(tok[:, pl.ds(off, quarter)], cot[...]) + tdot(
            sib[2 * j + dx, :, pl.ds(at, quarter)], sibcot[...]
        )

    def first(j):
        return (1, 0) if j % 2 == 0 else (0, 1)

    rs_in = {}

    def stage_a(j):
        da = first(j)
        near, far = (xn, yn) if j % 2 == 0 else (yn, xn)
        sib_in[j, 1].wait_recv()
        if j % 2:
            sib_in[j, 0].wait_recv()
        rs_s[1, j] = part(j, 1, 1).astype(BF16)
        rs_in[1, j] = go(remote(rs_s.at[1, j], rs_r.at[1, j], rs_ss.at[1, j], rs_rs.at[1, j], near))
        rs_s[0, j] = part(j, *da).astype(BF16)
        rs_in[0, j] = go(remote(rs_s.at[0, j], rs_r.at[0, j], rs_ss.at[0, j], rs_rs.at[0, j], near))
        if j % 2 == 0:
            sib_in[j, 0].wait_recv()
        keep_b[j] = part(j, da[1], da[0])
        keep_own[j] = part(j, 0, 0)

    def stage_b(j):
        far = yn if j % 2 == 0 else xn
        rs_in[1, j].wait_recv()
        rs_s[2, j] = (keep_b[j] + rs_r[1, j].astype(F32)).astype(BF16)
        rs_in[2, j] = go(remote(rs_s.at[2, j], rs_r.at[2, j], rs_ss.at[2, j], rs_rs.at[2, j], far))

    z_in = {}

    def stage_z(j):
        rs_in[0, j].wait_recv()
        rs_in[2, j].wait_recv()
        total = keep_own[j] + rs_r[0, j].astype(F32) + rs_r[2, j].astype(F32)
        if j == nz - 1:
            return total
        z_s[j] = total.astype(BF16)
        z_in[j] = go(remote(z_s.at[j], z_r.at[j], z_ss.at[j], z_rs.at[j], zpeer[j]))
        return None

    for j in range(nz):
        stage_a(j)
    stage_b(0)
    for j in range(1, nz):
        stage_b(j)
        stage_z(j - 1)
    grad = stage_z(nz - 1)
    for j in range(nz - 1):
        z_in[j].wait_recv()
        grad = grad + z_r[j].astype(F32)
    g_q[0] = grad
    g_in = {
        2: go(remote(g_q.at[0], g_q.at[2], g_ss.at[2], g_rs.at[2], sibling)),
    }

    def update(gradient, dy, dc):
        at = pl.ds(pl.multiple_of((flip(c, dc) * 2 + flip(y, dy)) * quarter, BLOCK), quarter)
        new = adamw(wt[at, :], mo[at, :], ve[at, :], gradient)
        w_o[at, :], m_o[at, :], v_o[at, :] = new
        return new[0]

    for load in loads[6:]:
        load.wait()
    fresh = update(grad, 0, 0)
    row = lax.broadcasted_iota(jnp.int32, (TAIL, hd), 0)
    tail = jnp.zeros((TAIL, hd), F32)
    for b in range(blocks):
        piece = fresh[b * BLOCK : (b + 1) * BLOCK]
        peak = jnp.max(jnp.max(jnp.abs(piece), axis=0, keepdims=True), axis=1, keepdims=True)
        peak = peak + peak_eps
        ag[0, 0, nz - 1, b * BLOCK : (b + 1) * BLOCK] = (piece / peak).astype(BF16)
        rest = jnp.broadcast_to(peak, (TAIL, hd))
        for k in range(3):
            high = rest.astype(BF16).astype(F32)
            tail = jnp.where(row == 3 * b + k, high, tail)
            rest = rest - high
    ag[0, 0, nz - 1, quarter : quarter + TAIL] = tail.astype(BF16)

    az_in = {
        j: go(remote(ag.at[0, 0, nz - 1], ag.at[0, 0, j], az_ss.at[j], az_rs.at[j], zpeer[j]))
        for j in range(nz - 1)
    }
    raw = [jnp.zeros((steps * rows, hd), F32)]
    ap_in, as_in = {}, {}

    def place(dc, p, j):
        shard_at = lax.rem(z + nz - 1 - j, nz) * 2 + flip(x, p & 1)
        return shard_at * shard + (flip(c, dc) * 2 + flip(y, p >> 1)) * quarter

    def project(dc, p, j):
        at = place(dc, p, j)
        t = ag[dc, p, j, quarter : quarter + TAIL].astype(F32)
        for b in range(blocks):
            peak = t[3 * b : 3 * b + 1] + t[3 * b + 1 : 3 * b + 2] + t[3 * b + 2 : 3 * b + 3]
            h = hid[:, pl.ds(pl.multiple_of(at + b * BLOCK, BLOCK), BLOCK)]
            got = jnp.dot(
                h, ag[dc, p, j, b * BLOCK : (b + 1) * BLOCK], preferred_element_type=F32
            )
            raw[0] = raw[0] + got * peak

    def share(p, j):
        as_in[p, j] = go(
            remote(ag.at[0, p, j], ag.at[1, p, j], as_ss.at[p, j], as_rs.at[p, j], sibling)
        )

    def plane(src, p, j, where):
        ap_in[p, j] = go(
            remote(ag.at[0, src, j], ag.at[0, p, j], ap_ss.at[p - 1, j], ap_rs.at[p - 1, j], where)
        )

    def spread(j):
        if j < nz - 1:
            az_in[j].wait_recv()
        plane(0, 1, j, xn)
        plane(0, 2, j, yn)
        share(0, j)
        project(0, 0, j)

    def relay(j):
        ap_in[1, j].wait_recv()
        if j == 0:
            plane(1, 3, j, yn)
        share(1, j)
        ap_in[2, j].wait_recv()
        if j != 0:
            plane(2, 3, j, xn)
        share(2, j)
        project(0, 1, j)
        project(0, 2, j)

    def last(j):
        ap_in[3, j].wait_recv()
        share(3, j)
        project(0, 3, j)

    def cross(p, j):
        as_in[p, j].wait_recv()
        project(1, p, j)

    spread(nz - 1)
    g_in[1] = go(remote(g_q.at[0], g_q.at[1], g_ss.at[1], g_rs.at[1], yn))
    g_in[2].wait_recv()
    update(g_q[2], 0, 1)
    order = [nz - 1] + list(range(nz - 1))
    for i in range(1, nz):
        spread(order[i])
        relay(order[i - 1])
        cross(0, order[i - 1])
    g_in[1].wait_recv()
    g_in[3] = go(remote(g_q.at[1], g_q.at[3], g_ss.at[3], g_rs.at[3], sibling))
    update(g_q[1], 1, 0)
    relay(order[-1])
    g_in[3].wait_recv()
    update(g_q[3], 1, 1)
    for j in order:
        last(j)
    cross(0, order[-1])
    for p in (1, 2, 3):
        for j in order:
            cross(p, j)

    raw_o[...] = raw[0] * cosr + pltpu.roll(raw[0], hd // 2, 1) * sinr
    for copy in sends:
        copy.wait_send()


def finish_kernel(
    nz, w, m, v, ag, keys_ref, qs, ex, mx, sm, vc, nv,
    w_h, m_h, v_h, roll_h, fk_h, att_h, fk_o, att_o, o_s, t_s,
):
    f = lax.axis_index("fsdp")
    r = lax.axis_index("rep")
    z, x = lax.div(f, 2), lax.rem(f, 2)
    y, c = lax.div(r, 2), lax.rem(r, 2)
    shard, hd = w.shape
    quarter = shard // 4
    rows = qs.shape[0]
    steps = keys_ref.shape[0] // rows
    heads = qs.shape[1] // steps
    scale = 1.0 / math.sqrt(hd)

    def flip(value, bit):
        return 1 - value if bit else value

    outs = []
    for n, (a, b) in enumerate(((w, w_h), (m, m_h), (v, v_h))):
        outs.append(pltpu.make_async_copy(a, b, t_s.at[n]))
    for dc in range(2):
        for p in range(4):
            for j in range(nz):
                at = lax.rem(z + nz - 1 - j, nz) * 2 + flip(x, p & 1)
                at = at * shard + (flip(c, dc) * 2 + flip(y, p >> 1)) * quarter
                outs.append(
                    pltpu.make_async_copy(
                        ag.at[dc, p, j, pl.ds(0, quarter)],
                        roll_h.at[pl.ds(pl.multiple_of(at, BLOCK), quarter)],
                        o_s.at[(dc * 4 + p) * nz + j],
                    )
                )
    for copy in outs:
        copy.start()
    keys = keys_ref[...]
    keys = keys.astype(BF16)
    for s in range(steps):
        fk_o[s] = keys[s * rows : (s + 1) * rows]
    keys = keys.astype(F32)
    step_of = lax.broadcasted_iota(jnp.int32, (steps * heads, 1), 0) // heads
    lines = [[] for _ in range(steps)]
    for i in range(rows):
        query = qs[i]
        top_c = mx[i][:, :1]
        sum_c = sm[i][:, :1]
        top = top_c
        scf = []
        for t in range(steps):
            k = keys[t * rows + i : t * rows + i + 1]
            sc = jnp.sum(query * k, axis=1, keepdims=True) * scale
            sc = jnp.where(step_of >= t, sc, -jnp.inf)
            scf.append(sc)
            top = jnp.maximum(top, sc)
        exf = [jnp.exp(sc - top) for sc in scf]
        fix = jnp.exp(top_c - top)
        total = sum_c * fix
        for e in exf:
            total = total + e
        prob = (ex[i] * (fix / total)).astype(BF16)
        mixed = jnp.dot(prob, vc[i], preferred_element_type=F32)
        for t in range(steps):
            pf = (exf[t] / total).astype(BF16).astype(F32)
            mixed = mixed + pf * nv[t, i : i + 1, :].astype(F32)
        for s in range(steps):
            lines[s].append(
                jnp.concatenate(
                    [mixed[s * heads + h : s * heads + h + 1] for h in range(heads)], axis=1
                )
            )
    for s in range(steps):
        att_o[s] = jnp.concatenate(lines[s], axis=0).astype(BF16)
    for n, (a, b) in enumerate(((fk_o, fk_h), (att_o, att_h))):
        outs.append(pltpu.make_async_copy(a, b, t_s.at[3 + n]))
        outs[-1].start()
    for copy in outs:
        copy.wait()


def fused(
    nz, tokens_x, cotangent, master_weight, first_moment, second_moment,
    hidden_dec, queries, new_values, key_cache, value_cache, cache_lengths,
):
    steps, rows, width = hidden_dec.shape
    shard, hd = master_weight.shape
    quarter = shard // 4
    slots = key_cache.shape[1]
    qrows = queries.shape[2] // hd * steps
    tokens = tokens_x.shape[0]
    vm = pl.BlockSpec(memory_space=pltpu.VMEM)
    dma = pltpu.SemaphoreType.DMA
    shape = jax.ShapeDtypeStruct
    anyspace = pl.BlockSpec(memory_space=pltpu.HBM)
    vmem = pltpu.VMEM
    made = pl.pallas_call(
        functools.partial(step_kernel, nz),
        out_shape=(
            shape((shard, hd), F32), shape((shard, hd), F32), shape((shard, hd), F32),
            shape((2, 4, nz, quarter + TAIL, hd), BF16),
            shape((steps * rows, hd), F32),
            shape((rows, qrows, hd), F32),
            shape((rows, qrows, slots), F32),
            shape((rows, qrows, hd), F32),
            shape((rows, qrows, hd), F32),
            shape(value_cache.shape, BF16),
            shape(new_values.shape, BF16),
        ),
        in_specs=[anyspace] * 11,
        out_specs=(vm,) * 11,
        scratch_shapes=[
            vmem(tokens_x.shape, BF16), vmem(cotangent.shape, BF16),
            vmem((shard, hd), F32), vmem((shard, hd), F32), vmem((shard, hd), F32),
            vmem(hidden_dec.shape, BF16), vmem((steps * rows, width), BF16),
            vmem(queries.shape, BF16), vmem(key_cache.shape, BF16),
            pltpu.SMEM(cache_lengths.shape, jnp.int32), dma((11,)),
            vmem((2 * nz, tokens, shard // 2), BF16),
            vmem((tokens, hd), BF16),
            vmem((3, nz, quarter, hd), BF16),
            vmem((3, nz, quarter, hd), BF16),
            vmem((nz, quarter, hd), F32),
            vmem((nz, quarter, hd), F32),
            vmem((nz - 1, quarter, hd), BF16),
            vmem((nz - 1, quarter, hd), BF16),
            vmem((4, quarter, hd), F32),
            dma((2 * nz + 1,)), dma((2 * nz + 1,)),
            dma((3, nz)), dma((3, nz)),
            dma((nz - 1,)), dma((nz - 1,)),
            dma((4,)), dma((4,)),
            dma((nz - 1,)), dma((nz - 1,)),
            dma((3, nz)), dma((3, nz)),
            dma((4, nz)), dma((4, nz)),
        ],
        compiler_params=pltpu.CompilerParams(
            collective_id=0, has_side_effects=True, vmem_limit_bytes=40 * 1024 * 1024
        ),
        name="step",
    )(
        *(
            pltpu.with_memory_space_constraint(arg, pltpu.HBM)
            for arg in (
                tokens_x, cotangent, master_weight, first_moment, second_moment,
                hidden_dec, queries, new_values, key_cache, value_cache, cache_lengths,
            )
        )
    )
    return pl.pallas_call(
        functools.partial(finish_kernel, nz),
        out_shape=(
            shape((shard, hd), F32), shape((shard, hd), F32), shape((shard, hd), F32),
            shape((width, hd), BF16), shape(new_values.shape, BF16), shape(queries.shape, BF16),
        ),
        in_specs=[vm] * 11,
        out_specs=(anyspace,) * 6,
        scratch_shapes=[
            vmem(new_values.shape, BF16), vmem(queries.shape, BF16), dma((8 * nz,)), dma((5,)),
        ],
        compiler_params=pltpu.CompilerParams(vmem_limit_bytes=8 * 1024 * 1024),
        name="finish",
    )(*made)


def body(parts, replicas, *args):
    quarter, left = divmod(args[2].shape[0], 4)
    fits = replicas == 4 and parts >= 4 and parts % 2 == 0 and left == 0 and quarter % BLOCK == 0
    if fits and quarter // BLOCK * 3 <= TAIL:
        return fused(parts // 2, *args)
    return shards(*args)


def solution(mesh):
    return jax.shard_map(
        functools.partial(body, mesh.shape["fsdp"], mesh.shape["rep"]),
        mesh=mesh,
        in_specs=(
            P(("fsdp", "rep"), None),
            P(("fsdp", "rep"), None),
            P("fsdp", None),
            P("fsdp", None),
            P("fsdp", None),
            P(None, ("fsdp", "rep"), None),
            P(None, ("fsdp", "rep"), None),
            P(None, ("fsdp", "rep"), None),
            P(("fsdp", "rep"), None, None),
            P(("fsdp", "rep"), None, None),
            P(("fsdp", "rep")),
        ),
        out_specs=(
            P("fsdp", None),
            P("fsdp", None),
            P("fsdp", None),
            P(),
            P(None, ("fsdp", "rep"), None),
            P(None, ("fsdp", "rep"), None),
        ),
        check_vma=False,
    )
```

```python
import functools
import math

import jax
import jax.numpy as jnp
from jax import lax
from jax.experimental import pallas as pl
from jax.experimental.pallas import tpu as pltpu
from jax.sharding import PartitionSpec as P

D = 8192
BLOCK = 128


beta_one = 0.9
beta_two = 0.95
adam_eps = 1e-08
learn_rate = 0.0003
weight_decay = 0.1
step_count = 100
rope_theta = 1000000.0
peak_eps = 1e-06


def adamw(weight, first, second, gradient):
    first_new = beta_one * first + (1.0 - beta_one) * gradient
    second_new = beta_two * second + (1.0 - beta_two) * gradient * gradient
    first_hat = first_new / (1.0 - beta_one**step_count)
    second_hat = second_new / (1.0 - beta_two**step_count)
    weight_new = weight - learn_rate * (
        first_hat / (jnp.sqrt(second_hat) + adam_eps) + weight_decay * weight
    )
    return (weight_new, first_new, second_new)


def rotate(values, positions):
    half = values.shape[-1] // 2
    freq = rope_theta ** (-jnp.arange(half, dtype=jnp.float32) * 2.0 / values.shape[-1])
    angle = positions.astype(jnp.float32)[..., None] * freq
    cosine = jnp.cos(angle)
    sine = jnp.sin(angle)
    first_half = values[..., :half]
    second_half = values[..., half:]
    return jnp.concatenate(
        [first_half * cosine - second_half * sine, second_half * cosine + first_half * sine],
        axis=-1,
    )


def project_keys(hidden_size, quantized_weight, scales, lengths):
    decode_step_count, row_count, block_width = hidden_size.shape
    block_count = scales.shape[0]
    part_count = jnp.einsum(
        "qht,hti->qhi",
        hidden_size.reshape(decode_step_count * row_count, block_count, block_width // block_count),
        quantized_weight.reshape(block_count, block_width // block_count, -1),
        preferred_element_type=jnp.float32,
    )
    raw = jnp.sum(part_count * scales[None, :, None], axis=1).reshape(
        decode_step_count, row_count, -1
    )
    positions = lengths[None, :] + jnp.arange(decode_step_count, dtype=jnp.int32)[:, None]
    return rotate(raw, positions).astype(jnp.bfloat16)


def attend(query, cache_keys, cache_values, fresh, fresh_values, lengths):
    decode_step_count, row_count, joined = query.shape
    head_dim = cache_keys.shape[-1]
    heads = joined // head_dim
    valid = jnp.arange(cache_keys.shape[1], dtype=jnp.int32)[None, None, :] < lengths[:, None, None]
    outputs = []
    for section_index in range(decode_step_count):
        query_now = query[section_index].reshape(row_count, heads, head_dim)
        scores_c = jnp.einsum(
            "rhd,rcd->rhc", query_now, cache_keys, preferred_element_type=jnp.float32
        ) / math.sqrt(head_dim)
        scores_f = jnp.einsum(
            "rhd,trd->rht", query_now, fresh, preferred_element_type=jnp.float32
        ) / math.sqrt(head_dim)
        scores_c = jnp.where(valid, scores_c, -jnp.inf)
        scores_f = jnp.where(
            (jnp.arange(decode_step_count) <= section_index)[None, None, :], scores_f, -jnp.inf
        )
        peak = jnp.maximum(jnp.max(scores_c, axis=2), jnp.max(scores_f, axis=2))[:, :, None]
        exp_c = jnp.exp(scores_c - peak)
        exp_f = jnp.exp(scores_f - peak)
        total = jnp.sum(exp_c, axis=2, keepdims=True) + jnp.sum(exp_f, axis=2, keepdims=True)
        prob_c = (exp_c / total).astype(jnp.bfloat16)
        prob_f = (exp_f / total).astype(jnp.bfloat16)
        mixed = jnp.einsum("rhc,rcd->rhd", prob_c, cache_values, preferred_element_type=jnp.float32)
        mixed = mixed + jnp.einsum(
            "rht,trd->rhd", prob_f, fresh_values, preferred_element_type=jnp.float32
        )
        outputs.append(mixed.reshape(row_count, joined).astype(jnp.bfloat16))
    return jnp.stack(outputs)


def shards(
    tokens_x,
    cotangent,
    master_weight,
    first_moment,
    second_moment,
    hidden_dec,
    queries,
    new_values,
    key_cache,
    value_cache,
    cache_lengths,
):
    shard_rows = master_weight.shape[0]
    partial_grad = lax.psum_scatter(
        lax.dot_general(
            tokens_x, cotangent, (((0,), (0,)), ((), ())), preferred_element_type=jnp.float32
        ),
        "fsdp",
        scatter_dimension=0,
        tiled=True,
    )
    gradient = lax.psum(partial_grad, "rep")
    weight_next, first_next, second_next = adamw(
        master_weight, first_moment, second_moment, gradient
    )
    block_count = D // BLOCK
    row_ids = lax.axis_index("fsdp") * shard_rows + jnp.arange(shard_rows, dtype=jnp.int32)
    member = (row_ids // BLOCK)[:, None] == jnp.arange(block_count, dtype=jnp.int32)[None, :]
    row_peak = jnp.max(jnp.abs(weight_next), axis=1)
    local_peaks = jnp.max(jnp.where(member, row_peak[:, None], 0.0), axis=0)
    scales = lax.pmax(local_peaks, "fsdp") + peak_eps
    row_scale = jnp.sum(jnp.where(member, scales[None, :], 0.0), axis=1)
    local_quant = (weight_next / row_scale[:, None]).astype(jnp.bfloat16)
    rollout_weight = lax.all_gather(local_quant, "fsdp", axis=0, tiled=True)
    fresh_keys = project_keys(hidden_dec, rollout_weight, scales, cache_lengths)
    attended = attend(queries, key_cache, value_cache, fresh_keys, new_values, cache_lengths)
    return (weight_next, first_next, second_next, rollout_weight, fresh_keys, attended)


MESH = pl.DeviceIdType.MESH
F32 = jnp.float32
BF16 = jnp.bfloat16
ORDER = (3, 2, 1, 0)
TAIL = 16


def tdot(a, b):
    return lax.dot_general(a, b, (((0,), (0,)), ((), ())), preferred_element_type=F32)


def step_kernel(
    nz, tok_h, cot_h, wt_h, mo_h, ve_h, hid_h, qr_h, nv_h, kc_h, vc_h, lens_h,
    w_o, m_o, v_o, ag, raw_o, qs, ex, mx, sm, vc, nv,
    tok, cot, wt, mo, ve, hid3, hid, qr, kc, lens, in_s,
    sib, sibcot, rs_s, rs_r, z_s, z_r, g_q,
    sib_ss, sib_rs, rs_ss, rs_rs, z_ss, z_rs, g_ss, g_rs,
    az_ss, az_rs, ap_ss, ap_rs, as_ss, as_rs,
):
    f = lax.axis_index("fsdp")
    r = lax.axis_index("rep")
    z, x = lax.div(f, 2), lax.rem(f, 2)
    y, c = lax.div(r, 2), lax.rem(r, 2)
    shard = wt.shape[0]
    half = shard // 2
    quarter = shard // 4
    blocks = quarter // BLOCK
    steps, rows, joined = qr.shape
    hd = kc.shape[2]
    heads = joined // hd

    def flip(value, bit):
        return 1 - value if bit else value

    def zx(m):
        return flip(lax.div(z, 2), m >> 1) * 2 + flip(lax.rem(z, 2), m & 1)

    def device(m=0, dx=0, dy=0, dc=0):
        return {"fsdp": zx(m) * 2 + flip(x, dx), "rep": flip(y, dy) * 2 + flip(c, dc)}

    def remote(src, dst, ss, rs, where):
        return pltpu.make_async_remote_copy(
            src_ref=src, dst_ref=dst, send_sem=ss, recv_sem=rs,
            device_id=where, device_id_type=MESH,
        )

    sibling = device(dc=1)
    xn, yn, diag = device(dx=1), device(dy=1), device(dx=1, dy=1)
    zpeer = {1: device(m=1), 2: device(m=2)}
    barrier = pltpu.get_barrier_semaphore()
    peers = [sibling, xn, yn, zpeer[1], zpeer[2], diag]
    for peer in peers:
        pl.semaphore_signal(barrier, inc=1, device_id=peer, device_id_type=MESH)

    loads = [
        pltpu.make_async_copy(a, b, in_s.at[n])
        for n, (a, b) in enumerate((
            (tok_h, tok), (cot_h, cot), (qr_h, qr), (kc_h, kc), (lens_h, lens), (hid_h, hid3),
            (wt_h, wt), (mo_h, mo), (ve_h, ve), (vc_h, vc), (nv_h, nv),
        ))
    ]
    for load in loads:
        load.start()
    pl.semaphore_wait(barrier, len(peers))

    def target(j):
        return zx(ORDER[j])

    sends = []

    def go(copy):
        copy.start()
        sends.append(copy)
        return copy

    cot_in = go(remote(cot_h, sibcot, sib_ss.at[2 * nz], sib_rs.at[2 * nz], sibling))
    sib_in = {}
    for j in range(nz):
        for dx in (1, 0):
            k = 2 * j + dx
            off = pl.multiple_of((target(j) * 2 + flip(x, dx)) * shard + (1 - c) * half, BLOCK)
            sib_in[j, dx] = go(
                remote(tok_h.at[:, pl.ds(off, half)], sib.at[k], sib_ss.at[k], sib_rs.at[k], sibling)
            )
    cot_in.wait_recv()
    loads[0].wait()
    loads[1].wait()

    def part(j, dx, dy):
        at = flip(y, dy) * quarter
        off = pl.multiple_of((target(j) * 2 + flip(x, dx)) * shard + c * half + at, BLOCK)
        at = pl.multiple_of(at, BLOCK)
        return tdot(tok[:, pl.ds(off, quarter)], cot[...]) + tdot(
            sib[2 * j + dx, :, pl.ds(at, quarter)], sibcot[...]
        )

    def first(j):
        return (1, 0) if j % 2 == 0 else (0, 1)

    rs_in = {}

    def stage_a(j):
        sib_in[j, 1].wait_recv()
        for n, dx, dy, where in ((1, 1, 1, diag), (0, 1, 0, xn), (2, 0, 1, yn)):
            if n == 2:
                sib_in[j, 0].wait_recv()
            rs_s[n, j] = part(j, dx, dy).astype(BF16)
            rs_in[n, j] = go(
                remote(rs_s.at[n, j], rs_r.at[n, j], rs_ss.at[n, j], rs_rs.at[n, j], where)
            )

    z_in = {}

    def stage_z(j):
        mine = part(j, 0, 0)
        rs_in[0, j].wait_recv()
        rs_in[1, j].wait_recv()
        rs_in[2, j].wait_recv()
        total = mine + rs_r[0, j].astype(F32) + rs_r[1, j].astype(F32) + rs_r[2, j].astype(F32)
        if j == nz - 1:
            return total
        if ORDER[j] == 2:
            z_in[0].wait_recv()
            total = total + z_r[0].astype(F32)
        z_s[j] = total.astype(BF16)
        where = zpeer[2 if ORDER[j] == 2 else 1]
        z_in[j] = go(remote(z_s.at[j], z_r.at[j], z_ss.at[j], z_rs.at[j], where))
        return None

    for j in range(nz):
        stage_a(j)
    for j in range(nz - 1):
        stage_z(j)
    for load in loads[2:6]:
        load.wait()

    scale = 1.0 / math.sqrt(hd)
    for i in range(rows):
        for s in range(steps):
            for h in range(heads):
                qs[i, s * heads + h : s * heads + h + 1, :] = qr[
                    s, i : i + 1, h * hd : (h + 1) * hd
                ].astype(F32)
    for i in range(rows):
        sc = lax.dot_general(
            qs[i].astype(BF16), kc[i], (((1,), (1,)), ((), ())), preferred_element_type=F32
        ) * scale
        slot = lax.broadcasted_iota(jnp.int32, sc.shape, 1)
        sc = jnp.where(slot < lens[i], sc, -jnp.inf)
        top = jnp.max(sc, axis=1, keepdims=True)
        e = jnp.exp(sc - top)
        ex[i] = e
        mx[i] = jnp.broadcast_to(top, mx.shape[1:])
        sm[i] = jnp.broadcast_to(jnp.sum(e, axis=1, keepdims=True), sm.shape[1:])

    grad = stage_z(nz - 1)
    for j in range(1, nz - 1):
        z_in[j].wait_recv()
        grad = grad + z_r[j].astype(F32)
    g_q[0] = grad
    g_in = {
        1: go(remote(g_q.at[0], g_q.at[1], g_ss.at[1], g_rs.at[1], yn)),
        2: go(remote(g_q.at[0], g_q.at[2], g_ss.at[2], g_rs.at[2], sibling)),
    }

    def update(gradient, dy, dc):
        at = pl.ds(pl.multiple_of((flip(c, dc) * 2 + flip(y, dy)) * quarter, BLOCK), quarter)
        new = adamw(wt[at, :], mo[at, :], ve[at, :], gradient)
        w_o[at, :], m_o[at, :], v_o[at, :] = new
        return new[0]

    for load in loads[6:]:
        load.wait()
    fresh = update(grad, 0, 0)
    def quantize(fresh, p):
        row = lax.broadcasted_iota(jnp.int32, (TAIL, hd), 0)
        tail = jnp.zeros((TAIL, hd), F32)
        for b in range(blocks):
            piece = fresh[b * BLOCK : (b + 1) * BLOCK]
            peak = jnp.max(jnp.max(jnp.abs(piece), axis=0, keepdims=True), axis=1, keepdims=True)
            peak = peak + peak_eps
            ag[0, p, nz - 1, b * BLOCK : (b + 1) * BLOCK] = (piece / peak).astype(BF16)
            rest = jnp.broadcast_to(peak, (TAIL, hd))
            for k in range(3):
                high = rest.astype(BF16).astype(F32)
                tail = jnp.where(row == 3 * b + k, high, tail)
                rest = rest - high
        ag[0, p, nz - 1, quarter : quarter + TAIL] = tail.astype(BF16)

    quantize(fresh, 0)
    az_in = {}

    def along(src, j, where):
        az_in[j] = go(
            remote(ag.at[0, 0, src], ag.at[0, 0, j], az_ss.at[j], az_rs.at[j], zpeer[where])
        )

    along(nz - 1, 1, 2)
    along(nz - 1, 2, 1)
    hid[...] = jnp.concatenate([hid3[s].astype(F32) for s in range(steps)], axis=0).astype(BF16)
    row = lax.broadcasted_iota(jnp.int32, (steps * rows, hd), 0)
    lane = lax.broadcasted_iota(jnp.int32, (steps * rows, hd), 1)
    position = row // rows
    for i in range(rows):
        position = position + jnp.where(row % rows == i, lens[i], 0)
    freq = jnp.exp((lane % (hd // 2)).astype(F32) * (-2.0 * math.log(rope_theta) / hd))
    angle = position.astype(F32) * freq
    cosr = jnp.cos(angle)
    sine = jnp.sin(angle)
    sinr = jnp.where(lane < hd // 2, -sine, sine)

    raw = [jnp.zeros((steps * rows, hd), F32)]
    ap_in, as_in = {}, {}

    def place(dc, p, j):
        shard_at = zx(ORDER[j]) * 2 + flip(x, p & 1)
        return shard_at * shard + (flip(c, dc) * 2 + flip(y, p >> 1)) * quarter

    def project(dc, p, j):
        at = place(dc, p, j)
        t = ag[dc, p, j, quarter : quarter + TAIL].astype(F32)
        for b in range(blocks):
            peak = t[3 * b : 3 * b + 1] + t[3 * b + 1 : 3 * b + 2] + t[3 * b + 2 : 3 * b + 3]
            h = hid[:, pl.ds(pl.multiple_of(at + b * BLOCK, BLOCK), BLOCK)]
            got = jnp.dot(
                h, ag[dc, p, j, b * BLOCK : (b + 1) * BLOCK], preferred_element_type=F32
            )
            raw[0] = raw[0] + got * peak

    def share(p, j):
        as_in[p, j] = go(
            remote(ag.at[0, p, j], ag.at[1, p, j], as_ss.at[p, j], as_rs.at[p, j], sibling)
        )

    def plane(src, p, j, where):
        ap_in[p, j] = go(
            remote(ag.at[0, src, j], ag.at[0, p, j], ap_ss.at[p - 1, j], ap_rs.at[p - 1, j], where)
        )

    def spread(j):
        if j < nz - 1:
            az_in[j].wait_recv()
        if j == 1:
            along(1, 0, 1)
        plane(0, 3, j, diag)
        plane(0, 1, j, xn)
        if j != nz - 1:
            plane(0, 2, j, yn)
        share(0, j)
        project(0, 0, j)

    def relay(j):
        ap_in[1, j].wait_recv()
        share(1, j)
        if j != nz - 1:
            ap_in[2, j].wait_recv()
        else:
            g_in[1].wait_recv()
            g_in[3] = go(remote(g_q.at[1], g_q.at[3], g_ss.at[3], g_rs.at[3], sibling))
            quantize(update(g_q[1], 1, 0), 2)
        share(2, j)
        project(0, 1, j)
        project(0, 2, j)

    def last(j):
        ap_in[3, j].wait_recv()
        share(3, j)
        project(0, 3, j)

    def cross(p, j):
        as_in[p, j].wait_recv()
        project(1, p, j)

    spread(nz - 1)
    g_in[2].wait_recv()
    update(g_q[2], 0, 1)
    order = [3, 2, 1, 0]
    for i in range(1, nz):
        spread(order[i])
        relay(order[i - 1])
        cross(0, order[i - 1])
    relay(order[-1])
    g_in[3].wait_recv()
    update(g_q[3], 1, 1)
    for j in order:
        last(j)
    cross(0, order[-1])
    for p in (1, 2, 3):
        for j in order:
            cross(p, j)

    raw_o[...] = raw[0] * cosr + pltpu.roll(raw[0], hd // 2, 1) * sinr
    for copy in sends:
        copy.wait_send()


def finish_kernel(
    nz, w, m, v, ag, keys_ref, qs, ex, mx, sm, vc, nv,
    w_h, m_h, v_h, roll_h, fk_h, att_h, fk_o, att_o, o_s, t_s,
):
    f = lax.axis_index("fsdp")
    r = lax.axis_index("rep")
    z, x = lax.div(f, 2), lax.rem(f, 2)
    y, c = lax.div(r, 2), lax.rem(r, 2)
    shard, hd = w.shape
    quarter = shard // 4
    rows = qs.shape[0]
    steps = keys_ref.shape[0] // rows
    heads = qs.shape[1] // steps
    scale = 1.0 / math.sqrt(hd)

    def flip(value, bit):
        return 1 - value if bit else value

    def zx(mask):
        return flip(lax.div(z, 2), mask >> 1) * 2 + flip(lax.rem(z, 2), mask & 1)

    outs = []
    for n, (a, b) in enumerate(((w, w_h), (m, m_h), (v, v_h))):
        outs.append(pltpu.make_async_copy(a, b, t_s.at[n]))
    for dc in range(2):
        for p in range(4):
            for j in range(nz):
                at = zx(ORDER[j]) * 2 + flip(x, p & 1)
                at = at * shard + (flip(c, dc) * 2 + flip(y, p >> 1)) * quarter
                outs.append(
                    pltpu.make_async_copy(
                        ag.at[dc, p, j, pl.ds(0, quarter)],
                        roll_h.at[pl.ds(pl.multiple_of(at, BLOCK), quarter)],
                        o_s.at[(dc * 4 + p) * nz + j],
                    )
                )
    for copy in outs:
        copy.start()
    keys = keys_ref[...]
    keys = keys.astype(BF16)
    for s in range(steps):
        fk_o[s] = keys[s * rows : (s + 1) * rows]
    keys = keys.astype(F32)
    step_of = lax.broadcasted_iota(jnp.int32, (steps * heads, 1), 0) // heads
    lines = [[] for _ in range(steps)]
    for i in range(rows):
        query = qs[i]
        top_c = mx[i][:, :1]
        sum_c = sm[i][:, :1]
        top = top_c
        scf = []
        for t in range(steps):
            k = keys[t * rows + i : t * rows + i + 1]
            sc = jnp.sum(query * k, axis=1, keepdims=True) * scale
            sc = jnp.where(step_of >= t, sc, -jnp.inf)
            scf.append(sc)
            top = jnp.maximum(top, sc)
        exf = [jnp.exp(sc - top) for sc in scf]
        fix = jnp.exp(top_c - top)
        total = sum_c * fix
        for e in exf:
            total = total + e
        prob = (ex[i] * (fix / total)).astype(BF16)
        mixed = jnp.dot(prob, vc[i], preferred_element_type=F32)
        for t in range(steps):
            pf = (exf[t] / total).astype(BF16).astype(F32)
            mixed = mixed + pf * nv[t, i : i + 1, :].astype(F32)
        for s in range(steps):
            lines[s].append(
                jnp.concatenate(
                    [mixed[s * heads + h : s * heads + h + 1] for h in range(heads)], axis=1
                )
            )
    for s in range(steps):
        att_o[s] = jnp.concatenate(lines[s], axis=0).astype(BF16)
    for n, (a, b) in enumerate(((fk_o, fk_h), (att_o, att_h))):
        outs.append(pltpu.make_async_copy(a, b, t_s.at[3 + n]))
        outs[-1].start()
    for copy in outs:
        copy.wait()


def fused(
    nz, tokens_x, cotangent, master_weight, first_moment, second_moment,
    hidden_dec, queries, new_values, key_cache, value_cache, cache_lengths,
):
    steps, rows, width = hidden_dec.shape
    shard, hd = master_weight.shape
    quarter = shard // 4
    slots = key_cache.shape[1]
    qrows = queries.shape[2] // hd * steps
    tokens = tokens_x.shape[0]
    vm = pl.BlockSpec(memory_space=pltpu.VMEM)
    dma = pltpu.SemaphoreType.DMA
    shape = jax.ShapeDtypeStruct
    anyspace = pl.BlockSpec(memory_space=pltpu.HBM)
    vmem = pltpu.VMEM
    made = pl.pallas_call(
        functools.partial(step_kernel, nz),
        out_shape=(
            shape((shard, hd), F32), shape((shard, hd), F32), shape((shard, hd), F32),
            shape((2, 4, nz, quarter + TAIL, hd), BF16),
            shape((steps * rows, hd), F32),
            shape((rows, qrows, hd), F32),
            shape((rows, qrows, slots), F32),
            shape((rows, qrows, hd), F32),
            shape((rows, qrows, hd), F32),
            shape(value_cache.shape, BF16),
            shape(new_values.shape, BF16),
        ),
        in_specs=[anyspace] * 11,
        out_specs=(vm,) * 11,
        scratch_shapes=[
            vmem(tokens_x.shape, BF16), vmem(cotangent.shape, BF16),
            vmem((shard, hd), F32), vmem((shard, hd), F32), vmem((shard, hd), F32),
            vmem(hidden_dec.shape, BF16), vmem((steps * rows, width), BF16),
            vmem(queries.shape, BF16), vmem(key_cache.shape, BF16),
            pltpu.SMEM(cache_lengths.shape, jnp.int32), dma((11,)),
            vmem((2 * nz, tokens, shard // 2), BF16),
            vmem((tokens, hd), BF16),
            vmem((3, nz, quarter, hd), BF16),
            vmem((3, nz, quarter, hd), BF16),
            vmem((nz - 1, quarter, hd), BF16),
            vmem((nz - 1, quarter, hd), BF16),
            vmem((4, quarter, hd), F32),
            dma((2 * nz + 1,)), dma((2 * nz + 1,)),
            dma((3, nz)), dma((3, nz)),
            dma((nz - 1,)), dma((nz - 1,)),
            dma((4,)), dma((4,)),
            dma((nz - 1,)), dma((nz - 1,)),
            dma((3, nz)), dma((3, nz)),
            dma((4, nz)), dma((4, nz)),
        ],
        compiler_params=pltpu.CompilerParams(
            collective_id=0, has_side_effects=True, vmem_limit_bytes=40 * 1024 * 1024
        ),
        name="step",
    )(
        *(
            pltpu.with_memory_space_constraint(arg, pltpu.HBM)
            for arg in (
                tokens_x, cotangent, master_weight, first_moment, second_moment,
                hidden_dec, queries, new_values, key_cache, value_cache, cache_lengths,
            )
        )
    )
    return pl.pallas_call(
        functools.partial(finish_kernel, nz),
        out_shape=(
            shape((shard, hd), F32), shape((shard, hd), F32), shape((shard, hd), F32),
            shape((width, hd), BF16), shape(new_values.shape, BF16), shape(queries.shape, BF16),
        ),
        in_specs=[vm] * 11,
        out_specs=(anyspace,) * 6,
        scratch_shapes=[
            vmem(new_values.shape, BF16), vmem(queries.shape, BF16), dma((8 * nz,)), dma((5,)),
        ],
        compiler_params=pltpu.CompilerParams(vmem_limit_bytes=8 * 1024 * 1024),
        name="finish",
    )(*made)


def body(parts, replicas, *args):
    quarter, left = divmod(args[2].shape[0], 4)
    fits = replicas == 4 and parts == 2 * len(ORDER) and left == 0 and quarter % BLOCK == 0
    if fits and quarter // BLOCK * 3 <= TAIL:
        return fused(parts // 2, *args)
    return shards(*args)


def solution(mesh):
    return jax.shard_map(
        functools.partial(body, mesh.shape["fsdp"], mesh.shape["rep"]),
        mesh=mesh,
        in_specs=(
            P(("fsdp", "rep"), None),
            P(("fsdp", "rep"), None),
            P("fsdp", None),
            P("fsdp", None),
            P("fsdp", None),
            P(None, ("fsdp", "rep"), None),
            P(None, ("fsdp", "rep"), None),
            P(None, ("fsdp", "rep"), None),
            P(("fsdp", "rep"), None, None),
            P(("fsdp", "rep"), None, None),
            P(("fsdp", "rep")),
        ),
        out_specs=(
            P("fsdp", None),
            P("fsdp", None),
            P("fsdp", None),
            P(),
            P(None, ("fsdp", "rep"), None),
            P(None, ("fsdp", "rep"), None),
        ),
        check_vma=False,
    )
```
